32 devices in a mesh: band: 8 (over z, y), col: 4 (over x, core).
Axes of the slice: x: 2, y: 2, z: 4, core: 2. Of those that a mesh axis runs over, the one named last changes fastest.
Arguments:
- valence_wave: bfloat16 [16, 96, 9216], P('band', 'col'), may hold values from -6 to 6
- conduction_wave: bfloat16 [8, 96, 9216], P('band', 'col'), may hold values from -6 to 6
- valence_index: int32 [16], replicated, may hold values from 0 to 4095
- occupied_energy: float32 [4096], replicated, may hold values from -6 to -0.5
- conduction_energy: float32 [8], replicated, may hold values from 0.5 to 8
- frequency: float32 [4], replicated, may hold values from 0.5 to 16
- gvec_cell: int32 [8192], P('col'), may hold values from 0 to 221183, as said below
- block_cell: int32 [16], P('col'), may hold values from 0 to 221183, as said below
Outputs:
- chi: float32 [8192, 128], P(('col', 'band'))
The draws below stay inside these ranges and needn't reach their ends.
Inputs may be any that keep to these rules, and one draw needn't show every extreme that they name: `gvec_cell`: for rows j of owner k (k * 2048 <= j < (k + 1) * 2048) the entry is (kx 24 + ky - k * 24) * 96 + kz for the G vector's grid point (kx, ky, kz), whose ky lies in [k * 24, (k + 1) * 24); no point appears twice among the rows and block columns of one owner. `block_cell`: block column m has owner k = m // 4 and is encoded as for gvec_cell; its points differ from every row point of the same owner.
All inputs are finite; a program needn't handle non-finite values.
Results may differ from the reference program's by a relative error of at most 0.018.
Values may be sent and summed in bfloat16 or wider, within the bound.
A program may use at most 192 MiB of HBM per device.

```python
import math
import jax
import jax.numpy as jnp
from jax import lax

GX = 96
GY = 96
GZ = 96
G_DEV = 2048
NV = 16
NW = 4
NOCC = 4096
GB = 16
NG = 8192
NC = 8
PENCIL = 221184
GB_DEV = 4


def cell_lists(key):
    owners = NG // G_DEV
    keys = jax.random.split(jax.random.fold_in(key, 7), owners)
    return jax.vmap(lambda single: jax.random.permutation(single, PENCIL))(keys)


def draw_gvec_cell(key, part):
    lists = cell_lists(key)
    return lists[:, :G_DEV].reshape(-1).astype(jnp.int32)


def draw_block_cell(key, part):
    lists = cell_lists(key)
    return lists[:, G_DEV:G_DEV + GB_DEV].reshape(-1).astype(jnp.int32)


def set_ends(values, stream_key, low, high):
    longest = values.shape.index(max(values.shape))
    spots = []
    for shift in (0, 1):
        where = [jax.random.randint(jax.random.fold_in(stream_key, axis), (), 0, length) for axis, length in enumerate(values.shape)]
        where[longest] = (where[longest] + shift) % values.shape[longest]
        spots.append(tuple(where))
    return values.at[spots[0]].set(low).at[spots[1]].set(high)


def shard_levels(rng, extent, cuts, smallest, largest):
    factor_of, own = 1.0, jax.random.fold_in(rng, 6)
    for dim, parts in cuts:
        steps = jnp.exp(jax.random.uniform(jax.random.fold_in(own, dim), (parts,), jnp.float32, smallest / len(cuts), largest / len(cuts)))
        factor_of = factor_of * jnp.repeat(steps, extent[dim] // parts).reshape([-1 if axis == dim else 1 for axis in range(len(extent))])
    return factor_of


def bell_draw(stream_key, shape, scale, bound, cuts=(), kind=jnp.bfloat16):
    entries = jax.random.normal(stream_key, shape, jnp.float32) * scale
    if len(cuts) > 0:
        entries = shard_levels(stream_key, shape, cuts, -0.22, 0.18) * entries
    return jnp.clip(entries, min=-bound, max=bound).astype(kind)


def setup_inputs(seed: int = 0) -> dict:
    streams_of = jax.random.split(jax.random.key(seed), 9)
    return {
        "valence_wave": bell_draw(streams_of[0], (NV, GX, GY * GZ), 1.0, 6.0, ((0, 8), (1, 4))),
        "conduction_wave": bell_draw(streams_of[1], (NC, GX, GY * GZ), 1.0, 6.0, ((0, 8), (1, 4))),
        "valence_index": set_ends(jax.random.randint(streams_of[2], (NV,), 0, NOCC), jax.random.fold_in(streams_of[2], 1), 0, NOCC - 1).astype(jnp.int32),
        "occupied_energy": jnp.clip(jax.random.uniform(streams_of[3], (NOCC,), jnp.float32, -6.0, -0.5), -6.0, -0.5),
        "conduction_energy": jnp.clip(jax.random.uniform(streams_of[4], (NC,), jnp.float32, 0.5, 8.0), 0.5, 8.0),
        "frequency": jnp.clip(jnp.exp(jax.random.uniform(streams_of[5], (NW,), jnp.float32, math.log(0.5), math.log(16.0))), 0.5, 16.0),
        "gvec_cell": draw_gvec_cell(jax.random.fold_in(streams_of[8], 71), 0),
        "block_cell": draw_block_cell(jax.random.fold_in(streams_of[8], 71), 0),
    }


HIGHEST = lax.Precision.HIGHEST

def dft_tables(length, factor, out_type):
    indices = jnp.arange(length, dtype=jnp.int32)
    phases = indices[:, None] * indices[None, :] % length
    angles = phases.astype(jnp.float32) * (2.0 * math.pi / length)
    return ((jnp.cos(angles) * factor).astype(out_type), (-jnp.sin(angles) * factor).astype(out_type))

def weighted_columns(block, weights):
    columns = block.astype(jnp.float32)
    stacked = jnp.stack([columns, jnp.stack([-columns[1], columns[0]])])
    scaled = stacked[None] * weights[:, None, None, :, None]
    scaled = scaled.transpose(2, 3, 0, 1, 4).astype(jnp.bfloat16)
    return scaled.reshape(2, block.shape[1], -1)

def reference(valence_wave, conduction_wave, valence_index, occupied_energy, conduction_energy, frequency, gvec_cell, block_cell):
    col_count = NG // G_DEV
    slab_y = GY // col_count

    def grid_points(cells, per_owner):
        owner = jnp.arange(cells.shape[0], dtype=jnp.int32) // per_owner
        point_x = cells // (slab_y * GZ)
        point_y = owner * slab_y + cells // GZ % slab_y
        point_z = cells % GZ
        return (point_x, point_y, point_z)
    row_points = grid_points(gvec_cell, G_DEV)
    block_points = grid_points(block_cell, GB // col_count)
    x_cosine, x_sine = dft_tables(GX, 1.0 / math.sqrt(GX), jnp.bfloat16)
    cosine_full = x_cosine.astype(jnp.float32)
    sine_full = x_sine.astype(jnp.float32)
    valence_float = valence_wave.astype(jnp.float32).reshape(NV, GX, GY, GZ)

    def one_band(wave):
        products = valence_float * wave.astype(jnp.float32).reshape(GX, GY, GZ)[None]
        plane = jnp.fft.fft2(products, axes=(2, 3)) / math.sqrt(GY * GZ)
        plane_real = lax.optimization_barrier(jnp.real(plane).astype(jnp.bfloat16)).astype(jnp.float32)
        plane_imag = lax.optimization_barrier(jnp.imag(plane).astype(jnp.bfloat16)).astype(jnp.float32)
        real_part = jnp.einsum('kx,vxyz->vkyz', cosine_full, plane_real, precision=HIGHEST) - jnp.einsum('kx,vxyz->vkyz', sine_full, plane_imag, precision=HIGHEST)
        imag_part = jnp.einsum('kx,vxyz->vkyz', sine_full, plane_real, precision=HIGHEST) + jnp.einsum('kx,vxyz->vkyz', cosine_full, plane_imag, precision=HIGHEST)
        density_real = real_part.astype(jnp.bfloat16)
        density_imag = imag_part.astype(jnp.bfloat16)
        rows = jnp.stack([density_real[:, row_points[0], row_points[1], row_points[2]], density_imag[:, row_points[0], row_points[1], row_points[2]]])
        block = jnp.stack([density_real[:, block_points[0], block_points[1], block_points[2]], density_imag[:, block_points[0], block_points[1], block_points[2]]])
        return (rows, block)
    rows, blocks = lax.map(one_band, conduction_wave)
    row_density = jnp.transpose(rows, (1, 0, 2, 3)).reshape(2, NC * NV, NG)
    block_density = jnp.transpose(blocks, (1, 0, 2, 3)).reshape(2, NC * NV, GB)
    valence_energy = occupied_energy[valence_index]
    gap = (conduction_energy[:, None] - valence_energy[None, :]).reshape(-1)
    freq_column = frequency[:, None]
    weights = -4.0 * gap[None, :] / (gap[None, :] * gap[None, :] + freq_column * freq_column) * (1.0 / math.sqrt(NV * NC))
    right_side = weighted_columns(block_density, weights).reshape(2 * NC * NV, -1)
    left_side = jnp.transpose(row_density, (2, 0, 1)).reshape(NG, 2 * NC * NV)
    return jnp.dot(left_side, right_side, preferred_element_type=jnp.float32)
```

```python
import math

import jax
import jax.numpy as jnp
from jax import lax
from jax.sharding import PartitionSpec as P

GY = 96


def dft_tables(length, factor, out_type):
    indices = jnp.arange(length, dtype=jnp.int32)
    phases = indices[:, None] * indices[None, :] % length
    angles = phases.astype(jnp.float32) * (2.0 * math.pi / length)
    return (
        (jnp.cos(angles) * factor).astype(out_type),
        (-jnp.sin(angles) * factor).astype(out_type),
    )


def weighted_columns(block, weights):
    columns = block.astype(jnp.float32)
    stacked = jnp.stack([columns, jnp.stack([-columns[1], columns[0]])])
    scaled = stacked[None] * weights[:, None, None, :, None]
    scaled = scaled.transpose(2, 3, 0, 1, 4).astype(jnp.bfloat16)
    return scaled.reshape(2, block.shape[1], -1)


def phase_tables(rows, cols, length, factor, out_type):
    phases = rows[:, None] * cols[None, :] % length
    angles = phases.astype(jnp.float32) * (2.0 * math.pi / length)
    return (
        (jnp.cos(angles) * factor).astype(out_type),
        (-jnp.sin(angles) * factor).astype(out_type),
    )


def one_hot(indices, length):
    span = jnp.arange(length, dtype=jnp.int32)
    return (indices[..., None] == span).astype(jnp.bfloat16)


def per_device(
    valence_wave,
    conduction_wave,
    valence_index,
    occupied_energy,
    conduction_energy,
    frequency,
    gvec_cell,
    block_cell,
):
    local_valence, slab_x, plane_size = valence_wave.shape
    band_count = lax.axis_size("band")
    col_count = lax.axis_size("col")
    both = ("col", "band")
    grid_x = slab_x * col_count
    grid_y = GY
    grid_z = plane_size // grid_y
    slab = grid_y // col_count * grid_z
    total_conduction = conduction_energy.shape[0]
    total_valence = local_valence * band_count
    pairs = local_valence * total_conduction
    lanes = pairs * slab_x
    norm_factor = 1.0 / math.sqrt(total_valence * total_conduction)
    bf16, f32 = jnp.bfloat16, jnp.float32

    conduction_all = lax.all_gather(conduction_wave, "band", axis=0, tiled=True)
    products = (valence_wave.astype(f32)[:, None] * conduction_all.astype(f32)[None]).astype(bf16)
    products = products.reshape(lanes, plane_size).T.reshape(grid_y, grid_z, lanes)

    z_cosine, z_sine = dft_tables(grid_z, 1.0, bf16)
    y_cosine, y_sine = dft_tables(grid_y, 1.0 / math.sqrt(grid_y * grid_z), bf16)
    z_table = jnp.stack([z_cosine, z_sine])
    y_table = jnp.stack([jnp.stack([y_cosine, -y_sine]), jnp.stack([y_sine, y_cosine])])
    z_done = jnp.einsum("rkz,yzn->rkyn", z_table, products, preferred_element_type=f32).astype(bf16)
    planes = jnp.einsum("srjy,rkyn->sjkn", y_table, z_done, preferred_element_type=f32).astype(bf16)
    planes = planes.reshape(2, col_count, slab, lanes)

    lane = jnp.arange(lanes, dtype=jnp.int32)
    plane_of = lax.axis_index("col") * slab_x + lane % slab_x
    x_cosine, x_sine = phase_tables(
        jnp.arange(grid_x, dtype=jnp.int32), plane_of, grid_x, 1.0 / math.sqrt(grid_x), bf16
    )
    x_table = jnp.concatenate([x_cosine, x_sine], axis=1)
    fold = (lane[:, None] // slab_x == jnp.arange(pairs, dtype=jnp.int32)[None, :]).astype(bf16)

    def partial_density(cells):
        picked = jnp.einsum(
            "ogc,socn->sogn", one_hot(cells % slab, slab), planes, preferred_element_type=f32
        ).astype(bf16)
        factors = jnp.einsum(
            "ogk,km->ogm", one_hot(cells // slab, grid_x), x_table, preferred_element_type=f32
        ).astype(bf16)
        cosine = factors[..., :lanes].astype(f32)
        sine = factors[..., lanes:].astype(f32)
        real = picked[0].astype(f32)
        imag = picked[1].astype(f32)
        turned = (
            (cosine * real - sine * imag).astype(bf16),
            (sine * real + cosine * imag).astype(bf16),
        )
        return jnp.stack(
            [jnp.einsum("ogn,np->pog", part, fold, preferred_element_type=f32) for part in turned]
        )

    cells_all = lax.all_gather(gvec_cell, "col", axis=0)
    blocks_all = lax.all_gather(block_cell, "col", axis=0)
    block_part = partial_density(blocks_all).reshape(2, pairs, -1)
    row_part = partial_density(cells_all).astype(bf16).reshape(2, pairs, -1)

    block_parts = lax.all_gather(block_part, both, axis=0).reshape(
        col_count, band_count, 2, pairs, -1
    )
    block = jnp.sum(block_parts, axis=0).astype(bf16)
    block = block.transpose(1, 0, 2, 3).reshape(2, band_count * pairs, -1)
    pieces = row_part.reshape(2, pairs, col_count * band_count, -1).transpose(2, 0, 1, 3)
    received = lax.all_to_all(pieces, both, split_axis=0, concat_axis=0, tiled=True)
    received = received.reshape(col_count, band_count, 2, pairs, -1)
    rows = jnp.sum(received.astype(f32), axis=0).astype(bf16)
    rows = rows.transpose(1, 0, 2, 3).reshape(2, band_count * pairs, -1)

    occupied_range = jnp.arange(occupied_energy.shape[0], dtype=jnp.int32)
    valence_energy = jnp.sum(
        jnp.where(valence_index[:, None] == occupied_range[None, :], occupied_energy[None, :], 0.0),
        axis=1,
    )
    gap = (conduction_energy[None, :] - valence_energy[:, None]).reshape(1, -1)
    freq_column = frequency[:, None]
    weights = -4.0 * gap / (gap * gap + freq_column * freq_column) * norm_factor
    right_side = weighted_columns(block, weights)
    return jnp.einsum("rpg,rpc->gc", rows, right_side, preferred_element_type=jnp.float32)


def solution(mesh):
    return jax.shard_map(
        per_device,
        mesh=mesh,
        in_specs=(
            P("band", "col", None),
            P("band", "col", None),
            P(),
            P(),
            P(),
            P(),
            P("col"),
            P("col"),
        ),
        out_specs=P(("col", "band"), None),
        check_vma=False,
    )
```
